32 devices in a mesh: cp: 8 (over y, x, core), sp: 4 (over z).
Axes of the slice: x: 2, y: 2, z: 4, core: 2. Of those that a mesh axis runs over, the one named last changes fastest.
Arguments:
- queries: bfloat16 [3072, 2048], P(('cp', 'sp')), may hold values from -6 to 6
- key_vectors: bfloat16 [3072, 512], P(('cp', 'sp')), may hold values from -6 to 6
- value_matrix: bfloat16 [3072, 512], P(('cp', 'sp')), may hold values from -6 to 6
- span_order: int32 [8], replicated, may hold values from 0 to 7, each once
Outputs:
- attended: bfloat16 [3072, 2048], P(('cp', 'sp'))
The draws below stay inside these ranges and needn't reach their ends.
Inputs may be any that keep to these rules, and one draw needn't show every extreme that they name: `span_order`: each value appears exactly once.
All inputs are finite; a program needn't handle non-finite values.
Results may differ from the reference program's by a relative error of at most 0.0055.
Values may be sent and summed in bfloat16 or wider, within the bound.
A program may use at most 128 MiB of HBM per device.

```python
import jax
import jax.numpy as jnp
from jax import lax

QUERY_HEADS = 16
KEY_VALUE_HEADS = 4
HEAD_WIDTH = 128
TOK_DEV = 96
SEQUENCE_TOKENS = 3072
PAIRS = 8
N_CP = 8
N_SP = 4


def drawn_pair(key):
    key_query, key_seed = jax.random.split(key, 2)
    query_draw = jnp.clip(jax.random.normal(key_query, (SEQUENCE_TOKENS, QUERY_HEADS * HEAD_WIDTH), jnp.float32), -6.0, 6.0)
    key_sample = jnp.clip(jax.random.normal(key_seed, (SEQUENCE_TOKENS, KEY_VALUE_HEADS * HEAD_WIDTH), jnp.float32), -6.0, 6.0)
    return (query_draw.astype(jnp.bfloat16), key_sample.astype(jnp.bfloat16))


def draw_queries(key, part):
    return drawn_pair(jax.random.fold_in(key, 11))[0]


def draw_key_vectors(key, part):
    return drawn_pair(jax.random.fold_in(key, 11))[1]


def block_scale(rng, dims, shards, low, high):
    def one(axis_at, blocks):
        steps = jax.random.uniform(jax.random.fold_in(jax.random.fold_in(rng, 6), axis_at), (blocks,), jnp.float32, low / len(shards), high / len(shards))
        return jnp.repeat(jnp.exp(steps), dims[axis_at] // blocks).reshape((-1,) + (1,) * (len(dims) - axis_at - 1))

    level = one(*shards[0])
    for cut in shards[1:]:
        level = level * one(*cut)
    return level


def gaussian(key, shape, spread, limit, shards=(), kind=jnp.bfloat16):
    result = jax.random.normal(key, shape, jnp.float32) * spread
    if len(shards) > 0:
        result = block_scale(key, shape, shards, -0.22, 0.18) * result
    return jnp.clip(result, min=-limit, max=limit).astype(kind)


def setup_inputs(seed: int = 0) -> dict:
    seeds = jax.random.split(jax.random.key(seed), 5)
    queries = draw_queries(jax.random.fold_in(seeds[4], 71), 0)
    key_vectors = draw_key_vectors(jax.random.fold_in(seeds[4], 71), 0)
    value_matrix = gaussian(seeds[2], (SEQUENCE_TOKENS, KEY_VALUE_HEADS * HEAD_WIDTH), 1.0, 6.0, ((0, 32),))
    span_order = jax.random.permutation(seeds[3], PAIRS).astype(jnp.int32)
    return {"queries": queries, "key_vectors": key_vectors, "value_matrix": value_matrix, "span_order": span_order}


def span_position(row_ids, span_order, pair_count, span_rows):
    slot_ids = row_ids // span_rows
    pair_ids = slot_ids // 2
    picked = jnp.sum(jnp.where(pair_ids[:, None] == jnp.arange(pair_count, dtype=jnp.int32)[None, :], span_order[None, :], 0), axis=1).astype(jnp.int32)
    span_ids = jnp.where(slot_ids % 2 == 1, 2 * pair_count - 1 - picked, picked)
    return (span_ids * span_rows + row_ids % span_rows).astype(jnp.int32)


def reference(queries, key_vectors, value_matrix, span_order):
    total_rows = queries.shape[0]
    span_rows = TOK_DEV * N_SP // 2
    row_ids = jnp.arange(total_rows, dtype=jnp.int32)
    positions = span_position(row_ids, span_order, N_CP, span_rows)
    group_width = QUERY_HEADS // KEY_VALUE_HEADS
    block_row_list = 512 if total_rows % 512 == 0 else total_rows
    block_total = total_rows // block_row_list
    entry_list = jnp.arange(block_total * KEY_VALUE_HEADS, dtype=jnp.int32)

    def attend(single_entry):
        block_number = single_entry // KEY_VALUE_HEADS
        key_value_head = single_entry % KEY_VALUE_HEADS
        first_row = (block_number * block_row_list).astype(jnp.int32)
        query_blk = lax.dynamic_slice(queries, (first_row, (key_value_head * group_width * HEAD_WIDTH).astype(jnp.int32)), (block_row_list, group_width * HEAD_WIDTH))
        query_blk = query_blk.astype(jnp.float32).reshape(block_row_list, group_width, HEAD_WIDTH)
        key_blk = lax.dynamic_slice(key_vectors, (jnp.int32(0), (key_value_head * HEAD_WIDTH).astype(jnp.int32)), (total_rows, HEAD_WIDTH)).astype(jnp.float32)
        value_blk = lax.dynamic_slice(value_matrix, (jnp.int32(0), (key_value_head * HEAD_WIDTH).astype(jnp.int32)), (total_rows, HEAD_WIDTH)).astype(jnp.float32)
        query_pos = lax.dynamic_slice(positions, (first_row,), (block_row_list,))
        scores = jnp.einsum("qhd,kd->hqk", query_blk, key_blk) * (HEAD_WIDTH ** -0.5)
        allowed = positions[None, None, :] <= query_pos[None, :, None]
        row_max = jnp.max(jnp.where(allowed, scores, -1e30), axis=2)
        weights = jnp.where(allowed, jnp.exp(scores - row_max[:, :, None]), 0.0)
        row_sum = jnp.sum(weights, axis=2)
        rounded = lax.optimization_barrier(weights.astype(jnp.bfloat16)).astype(jnp.float32)
        summed = jnp.einsum("hqk,kd->qhd", rounded, value_blk)
        return (summed / jnp.transpose(row_sum)[:, :, None]).astype(jnp.bfloat16)

    output_list = lax.map(attend, entry_list)
    output_list = output_list.reshape(block_total, KEY_VALUE_HEADS, block_row_list, group_width, HEAD_WIDTH)
    return jnp.transpose(output_list, (0, 2, 1, 3, 4)).reshape(total_rows, QUERY_HEADS * HEAD_WIDTH)
```

```python
import functools
import math

import jax
import jax.numpy as jnp
from jax import lax
from jax.experimental import pallas as pl
from jax.experimental.pallas import tpu as pltpu
from jax.sharding import PartitionSpec as P

HEAD_WIDTH = 128
MASKED = -1e30
MESH = pl.DeviceIdType.MESH


def forward_dims(kind, offset, dims):
    order = list(range(1, dims)) + [0] if kind == 0 else list(range(dims - 1, 0, -1)) + [0]
    last = max([order.index(b) for b in range(dims) if offset >> b & 1], default=-1)
    return order[last + 1 :]


def body(cp, sp, order_ref, q_ref, k_ref, v_ref, out_ref,
         qbuf, kbuf, vbuf, obuf, acc_e, acc_l,
         local_sem, zsend, zrecv, qsend, qrecv, csend, crecv, osend, orecv):
    dims = cp.bit_length() - 1
    c = lax.axis_index("cp")
    s = lax.axis_index("sp")
    tok = k_ref.shape[0]
    span = tok * sp // 2
    qcols = q_ref.shape[1] // sp
    heads = qcols // HEAD_WIDTH
    width = heads * span
    kv_src = (k_ref, v_ref)
    kv_buf = (kbuf, vbuf)

    peers = [(c, s ^ k) for k in range(1, sp)] + [(c ^ (1 << d), s) for d in range(dims)]
    barrier = pltpu.get_barrier_semaphore()
    for peer in peers:
        pl.semaphore_signal(barrier, inc=1, device_id=peer, device_id_type=MESH)

    def columns(index, size):
        return pl.ds(pl.multiple_of(index * size, size), size)

    def rows(index):
        return pl.ds(pl.multiple_of(index * tok, tok), tok)

    own = []
    for kind in range(2):
        own.append(pltpu.make_async_copy(
            kv_src[kind].at[:, columns(s, HEAD_WIDTH)],
            kv_buf[kind].at[c, rows(s), :], local_sem.at[kind]))
    own.append(pltpu.make_async_copy(q_ref.at[:, columns(s, qcols)], qbuf.at[s], local_sem.at[2]))
    for copy in own:
        copy.start()
    pl.semaphore_wait(barrier, len(peers))

    far_first = [k for k in range(sp // 2, sp)] + [k for k in range(1, sp // 2)]
    sends = []
    for k in far_first:
        for kind in range(2):
            copy = pltpu.make_async_remote_copy(
                src_ref=kv_src[kind].at[:, columns(s ^ k, HEAD_WIDTH)],
                dst_ref=kv_buf[kind].at[c, rows(s), :],
                send_sem=zsend.at[kind, k], recv_sem=zrecv.at[kind, k],
                device_id=(c, s ^ k), device_id_type=MESH)
            copy.start()
            sends.append(copy)
    q_copies = {}
    for k in far_first:
        copy = pltpu.make_async_remote_copy(
            src_ref=q_ref.at[:, columns(s ^ k, qcols)], dst_ref=qbuf.at[s],
            send_sem=qsend.at[k], recv_sem=qrecv.at[k],
            device_id=(c, s ^ k), device_id_type=MESH)
        copy.start()
        sends.append(copy)
        q_copies[k] = copy

    def z_wait(kind, k):
        piece = kv_buf[kind].at[c, rows(s ^ k), :]
        pltpu.make_async_remote_copy(
            src_ref=piece, dst_ref=piece, send_sem=zsend.at[kind, k], recv_sem=zrecv.at[kind, k],
            device_id=(c, s ^ k), device_id_type=MESH).wait_recv()

    def c_copy(kind, offset, k, dim):
        piece = kv_buf[kind].at[c ^ offset, rows(s ^ k), :]
        return pltpu.make_async_remote_copy(
            src_ref=piece, dst_ref=piece,
            send_sem=csend.at[kind, offset, k, dim],
            recv_sem=crecv.at[kind, offset ^ (1 << dim), k],
            device_id=(c ^ (1 << dim), s), device_id_type=MESH)

    def c_wait(kind, offset, k):
        piece = kv_buf[kind].at[c ^ offset, rows(s ^ k), :]
        pltpu.make_async_remote_copy(
            src_ref=piece, dst_ref=piece,
            send_sem=csend.at[kind, 0, k, 0], recv_sem=crecv.at[kind, offset, k],
            device_id=(c ^ 1, s), device_id_type=MESH).wait_recv()

    arrival = [0] + far_first
    events = []
    for offset in range(cp):
        for rank, k in enumerate(arrival):
            events.append((rank + 2 * bin(offset >> 1).count("1") + (offset & 1), offset & 1, offset, k))
    events.sort()
    for _, _, offset, k in events:
        for kind in range(2):
            if offset:
                c_wait(kind, offset, k)
            elif k:
                z_wait(kind, k)
            else:
                own[kind].wait()
            for dim in forward_dims(kind, offset, dims):
                copy = c_copy(kind, offset, k, dim)
                copy.start()
                sends.append(copy)
    own[2].wait()
    for k in far_first:
        q_copies[k].wait_recv()

    factor = math.log2(math.e) / math.sqrt(HEAD_WIDTH)
    half = sp // 2

    def gather_q(first):
        parts = []
        for h in range(heads):
            for j in range(half):
                parts.append(qbuf[first + j, :, h * HEAD_WIDTH : (h + 1) * HEAD_WIDTH])
        return jnp.concatenate(parts, axis=0).T

    qe = gather_q(0)
    ql = gather_q(half)

    def scores(key, query):
        return jnp.dot(key, query, preferred_element_type=jnp.float32)

    def peak(x):
        return jnp.max(x, axis=0, keepdims=True)

    def total(x):
        return jnp.sum(x, axis=0, keepdims=True)

    def weigh(x, top):
        return jnp.exp2(x * factor - top * factor)

    def mix(value, weights):
        return lax.dot_general(value, weights.astype(jnp.bfloat16), (((0,), (0,)), ((), ())),
                               preferred_element_type=jnp.float32)

    early = order_ref[c]
    key_e, key_l = kbuf[c, :span, :], kbuf[c, span:, :]
    val_e, val_l = vbuf[c, :span, :], vbuf[c, span:, :]
    allowed = lax.broadcasted_iota(jnp.int32, (span, width), 0) <= (
        lax.broadcasted_iota(jnp.int32, (span, width), 1) % span)
    x = jnp.where(allowed, scores(key_e, qe), MASKED)
    me = peak(x)
    w = weigh(x, me)
    le = total(w)
    acc_e[...] = mix(val_e, w)
    x1 = scores(key_e, ql)
    x2 = jnp.where(allowed, scores(key_l, ql), MASKED)
    ml = jnp.maximum(peak(x1), peak(x2))
    w1 = weigh(x1, ml)
    w2 = weigh(x2, ml)
    ll = total(w1) + total(w2)
    acc_l[...] = mix(val_e, w1) + mix(val_l, w2)

    def step(offset, state):
        me, le, ml, ll = state
        other = c ^ offset
        first = order_ref[other] < early
        key_e, key_l = kbuf[other, :span, :], kbuf[other, span:, :]
        val_e, val_l = vbuf[other, :span, :], vbuf[other, span:, :]
        x1 = scores(key_e, ql)
        x2 = scores(jnp.where(first, key_e, key_l), jnp.where(first, qe, ql))
        p1, p2 = peak(x1), peak(x2)
        new_l = jnp.maximum(jnp.maximum(ml, p1), jnp.where(first, ml, p2))
        new_e = jnp.where(first, jnp.maximum(me, p2), me)
        w1 = weigh(x1, new_l)
        w2 = weigh(x2, jnp.where(first, new_e, new_l))
        fe = jnp.exp2((me - new_e) * factor)
        fl = jnp.exp2((ml - new_l) * factor)
        t2 = total(w2)
        le = le * fe + jnp.where(first, t2, 0.0)
        ll = ll * fl + total(w1) + jnp.where(first, 0.0, t2)
        d1 = mix(val_e, w1)
        d2 = mix(jnp.where(first, val_e, val_l), w2)
        acc_e[...] = acc_e[...] * fe + jnp.where(first, d2, 0.0)
        acc_l[...] = acc_l[...] * fl + d1 + jnp.where(first, 0.0, d2)
        return (new_e, le, new_l, ll)

    me, le, ml, ll = lax.fori_loop(1, cp, step, (me, le, ml, ll))

    for first, acc, norm in ((0, acc_e, le), (half, acc_l, ll)):
        done = (acc[...] / norm).T.astype(jnp.bfloat16)
        for h in range(heads):
            for j in range(half):
                start = h * span + j * tok
                obuf[first + j, :, h * HEAD_WIDTH : (h + 1) * HEAD_WIDTH] = done[start : start + tok, :]
    last = pltpu.make_async_copy(obuf.at[s], out_ref.at[:, columns(s, qcols)], local_sem.at[3])
    last.start()
    o_copies = []
    for k in far_first:
        copy = pltpu.make_async_remote_copy(
            src_ref=obuf.at[s ^ k], dst_ref=out_ref.at[:, columns(s, qcols)],
            send_sem=osend.at[k], recv_sem=orecv.at[k],
            device_id=(c, s ^ k), device_id_type=MESH)
        copy.start()
        o_copies.append(copy)
    last.wait()
    for copy in o_copies:
        copy.wait()
    for copy in sends:
        copy.wait_send()


def per_device(queries, key_vectors, value_matrix, span_order):
    cp = lax.axis_size("cp")
    sp = lax.axis_size("sp")
    tok, q_width = queries.shape
    group = tok * sp
    qcols = q_width // sp
    width = qcols // HEAD_WIDTH * (group // 2)
    dims = cp.bit_length() - 1
    vmem = pl.BlockSpec(memory_space=pltpu.VMEM)
    dma = pltpu.SemaphoreType.DMA
    return pl.pallas_call(
        functools.partial(body, cp, sp),
        out_shape=jax.ShapeDtypeStruct((tok, q_width), jnp.bfloat16),
        in_specs=[pl.BlockSpec(memory_space=pltpu.SMEM), vmem, vmem, vmem],
        out_specs=vmem,
        scratch_shapes=[
            pltpu.VMEM((sp, tok, qcols), jnp.bfloat16),
            pltpu.VMEM((cp, group, HEAD_WIDTH), jnp.bfloat16),
            pltpu.VMEM((cp, group, HEAD_WIDTH), jnp.bfloat16),
            pltpu.VMEM((sp, tok, qcols), jnp.bfloat16),
            pltpu.VMEM((HEAD_WIDTH, width), jnp.float32),
            pltpu.VMEM((HEAD_WIDTH, width), jnp.float32),
            dma((4,)), dma((2, sp)), dma((2, sp)), dma((sp,)), dma((sp,)),
            dma((2, cp, sp, dims)), dma((2, cp, sp)), dma((sp,)), dma((sp,)),
        ],
        compiler_params=pltpu.CompilerParams(
            collective_id=0, has_side_effects=True, vmem_limit_bytes=60 * 1024 * 1024),
    )(span_order, queries, key_vectors, value_matrix)


def solution(mesh):
    return jax.shard_map(
        per_device,
        mesh=mesh,
        in_specs=(P(("cp", "sp"), None), P(("cp", "sp"), None), P(("cp", "sp"), None), P()),
        out_specs=P(("cp", "sp"), None),
        check_vma=False,
    )
```

```python
import functools
import math

import jax
import jax.numpy as jnp
from jax import lax
from jax.experimental import pallas as pl
from jax.experimental.pallas import tpu as pltpu
from jax.sharding import PartitionSpec as P

HEAD_WIDTH = 128
MASKED = -1e30
CHUNKS = 2
QUERY_AT = 8
UNROLL = 7
MESH = pl.DeviceIdType.MESH


def forward_dims(kind, offset, dims):
    order = list(range(1, dims)) + [0] if kind == 0 else list(range(dims - 1, 0, -1)) + [0]
    last = max([order.index(b) for b in range(dims) if offset >> b & 1], default=-1)
    return order[last + 1 :]


def body(cp, sp, order_ref, q_ref, k_ref, v_ref, out_ref,
         qbuf, kbuf, vbuf, obuf, acc_e, acc_l,
         local_sem, zsend, zrecv, qsend, qrecv, csend, crecv, osend, orecv):
    dims = cp.bit_length() - 1
    c = lax.axis_index("cp")
    s = lax.axis_index("sp")
    tok = k_ref.shape[0]
    span = tok * sp // 2
    qcols = q_ref.shape[1] // sp
    heads = qcols // HEAD_WIDTH
    chunks = CHUNKS
    ccols = qcols // chunks
    heads = heads // chunks
    width = heads * span
    kv_src = (k_ref, v_ref)
    kv_buf = (kbuf, vbuf)

    peers = [(c, s ^ k) for k in range(1, sp)] + [(c ^ (1 << d), s) for d in range(dims)]
    barrier = pltpu.get_barrier_semaphore()
    for peer in peers:
        pl.semaphore_signal(barrier, inc=1, device_id=peer, device_id_type=MESH)

    def columns(index, size):
        return pl.ds(pl.multiple_of(index * size, size), size)

    def rows(index):
        return pl.ds(pl.multiple_of(index * tok, tok), tok)

    own = []
    for kind in range(2):
        own.append(pltpu.make_async_copy(
            kv_src[kind].at[:, columns(s, HEAD_WIDTH)],
            kv_buf[kind].at[c, rows(s), :], local_sem.at[kind]))
    for chunk in range(chunks):
        own.append(pltpu.make_async_copy(
            q_ref.at[:, columns(s * chunks + chunk, ccols)], qbuf.at[chunk, s],
            local_sem.at[2 + chunk]))
    for copy in own:
        copy.start()
    pl.semaphore_wait(barrier, len(peers))

    far_first = [k for k in range(sp // 2, sp)] + [k for k in range(1, sp // 2)]
    sends = []
    for k in far_first:
        for kind in range(2):
            copy = pltpu.make_async_remote_copy(
                src_ref=kv_src[kind].at[:, columns(s ^ k, HEAD_WIDTH)],
                dst_ref=kv_buf[kind].at[c, rows(s), :],
                send_sem=zsend.at[kind, k], recv_sem=zrecv.at[kind, k],
                device_id=(c, s ^ k), device_id_type=MESH)
            copy.start()
            sends.append(copy)
    q_copies = []

    def send_queries():
        for chunk in range(chunks):
            for k in far_first:
                copy = pltpu.make_async_remote_copy(
                    src_ref=q_ref.at[:, columns((s ^ k) * chunks + chunk, ccols)],
                    dst_ref=qbuf.at[chunk, s],
                    send_sem=qsend.at[chunk, k], recv_sem=qrecv.at[chunk, k],
                    device_id=(c, s ^ k), device_id_type=MESH)
                copy.start()
                sends.append(copy)
                q_copies.append((chunk, copy))


    def z_wait(kind, k):
        piece = kv_buf[kind].at[c, rows(s ^ k), :]
        pltpu.make_async_remote_copy(
            src_ref=piece, dst_ref=piece, send_sem=zsend.at[kind, k], recv_sem=zrecv.at[kind, k],
            device_id=(c, s ^ k), device_id_type=MESH).wait_recv()

    def c_copy(kind, offset, k, dim):
        piece = kv_buf[kind].at[c ^ offset, rows(s ^ k), :]
        return pltpu.make_async_remote_copy(
            src_ref=piece, dst_ref=piece,
            send_sem=csend.at[kind, offset, k, dim],
            recv_sem=crecv.at[kind, offset ^ (1 << dim), k],
            device_id=(c ^ (1 << dim), s), device_id_type=MESH)

    def c_wait(kind, offset, k):
        piece = kv_buf[kind].at[c ^ offset, rows(s ^ k), :]
        pltpu.make_async_remote_copy(
            src_ref=piece, dst_ref=piece,
            send_sem=csend.at[kind, 0, k, 0], recv_sem=crecv.at[kind, offset, k],
            device_id=(c ^ 1, s), device_id_type=MESH).wait_recv()

    arrival = [0] + far_first
    events = []
    for offset in range(cp):
        for rank, k in enumerate(arrival):
            events.append((rank + 2 * bin(offset >> 1).count("1") + (offset & 1), offset & 1, offset, k))
    events.sort()
    for index, (_, _, offset, k) in enumerate(events):
        if index == min(QUERY_AT, len(events) - 1):
            send_queries()
        for kind in range(2):
            if offset:
                c_wait(kind, offset, k)
            elif k:
                z_wait(kind, k)
            else:
                own[kind].wait()
            for dim in forward_dims(kind, offset, dims):
                copy = c_copy(kind, offset, k, dim)
                copy.start()
                sends.append(copy)

    factor = math.log2(math.e) / math.sqrt(HEAD_WIDTH)
    half = sp // 2

    def gather_q(chunk, first):
        parts = []
        for h in range(heads):
            for j in range(half):
                parts.append(qbuf[chunk, first + j, :, h * HEAD_WIDTH : (h + 1) * HEAD_WIDTH])
        return jnp.concatenate(parts, axis=0).T

    def scores(key, query):
        return jnp.dot(key, query, preferred_element_type=jnp.float32)

    def peak(x):
        return jnp.max(x, axis=0, keepdims=True)

    def total(x):
        return jnp.sum(x, axis=0, keepdims=True)

    def weigh(x, top):
        return jnp.exp2(x * factor - top * factor)

    def mix(value, weights):
        return lax.dot_general(value, weights.astype(jnp.bfloat16), (((0,), (0,)), ((), ())),
                               preferred_element_type=jnp.float32)

    early = order_ref[c]
    key_e, key_l = kbuf[c, :span, :], kbuf[c, span:, :]
    val_e, val_l = vbuf[c, :span, :], vbuf[c, span:, :]
    allowed = lax.broadcasted_iota(jnp.int32, (span, width), 0) <= (
        lax.broadcasted_iota(jnp.int32, (span, width), 1) % span)

    def attend(chunk):
        qe = gather_q(chunk, 0)
        ql = gather_q(chunk, half)
        x = jnp.where(allowed, scores(key_e, qe), MASKED)
        me = peak(x)
        w = weigh(x, me)
        le = total(w)
        acc_e[...] = mix(val_e, w)
        x1 = scores(key_e, ql)
        x2 = jnp.where(allowed, scores(key_l, ql), MASKED)
        ml = jnp.maximum(peak(x1), peak(x2))
        w1 = weigh(x1, ml)
        w2 = weigh(x2, ml)
        ll = total(w1) + total(w2)
        acc_l[...] = mix(val_e, w1) + mix(val_l, w2)

        def step(offset, state):
            me, le, ml, ll = state
            other = c ^ offset
            first = order_ref[other] < early
            key_e, key_l = kbuf[other, :span, :], kbuf[other, span:, :]
            val_e, val_l = vbuf[other, :span, :], vbuf[other, span:, :]
            x1 = scores(key_e, ql)
            x2 = scores(jnp.where(first, key_e, key_l), jnp.where(first, qe, ql))
            p1, p2 = peak(x1), peak(x2)
            new_l = jnp.maximum(jnp.maximum(ml, p1), jnp.where(first, ml, p2))
            new_e = jnp.where(first, jnp.maximum(me, p2), me)
            w1 = weigh(x1, new_l)
            w2 = weigh(x2, jnp.where(first, new_e, new_l))
            fe = jnp.exp2((me - new_e) * factor)
            fl = jnp.exp2((ml - new_l) * factor)
            t2 = total(w2)
            le = le * fe + jnp.where(first, t2, 0.0)
            ll = ll * fl + total(w1) + jnp.where(first, 0.0, t2)
            d1 = mix(val_e, w1)
            d2 = mix(jnp.where(first, val_e, val_l), w2)
            acc_e[...] = acc_e[...] * fe + jnp.where(first, d2, 0.0)
            acc_l[...] = acc_l[...] * fl + d1 + jnp.where(first, 0.0, d2)
            return (new_e, le, new_l, ll)

        me, le, ml, ll = lax.fori_loop(1, cp, step, (me, le, ml, ll), unroll=UNROLL)

        for first, acc, norm in ((0, acc_e, le), (half, acc_l, ll)):
            done = (acc[...] / norm).T.astype(jnp.bfloat16)
            for h in range(heads):
                for j in range(half):
                    start = h * span + j * tok
                    obuf[chunk, first + j, :, h * HEAD_WIDTH : (h + 1) * HEAD_WIDTH] = done[start : start + tok, :]

    outs = []
    for chunk in range(chunks):
        own[2 + chunk].wait()
        for which, copy in q_copies:
            if which == chunk:
                copy.wait_recv()
        attend(chunk)
        place = columns(s * chunks + chunk, ccols)
        last = pltpu.make_async_copy(
            obuf.at[chunk, s], out_ref.at[:, place], local_sem.at[2 + chunks + chunk])
        last.start()
        outs.append(last)
        for k in far_first:
            copy = pltpu.make_async_remote_copy(
                src_ref=obuf.at[chunk, s ^ k], dst_ref=out_ref.at[:, place],
                send_sem=osend.at[chunk, k], recv_sem=orecv.at[chunk, k],
                device_id=(c, s ^ k), device_id_type=MESH)
            copy.start()
            outs.append(copy)
    for copy in outs:
        copy.wait()
    for copy in sends:
        copy.wait_send()


def per_device(queries, key_vectors, value_matrix, span_order):
    cp = lax.axis_size("cp")
    sp = lax.axis_size("sp")
    tok, q_width = queries.shape
    group = tok * sp
    qcols = q_width // sp
    width = qcols // HEAD_WIDTH // CHUNKS * (group // 2)
    dims = cp.bit_length() - 1
    anywhere = pl.BlockSpec(memory_space=pl.ANY)
    dma = pltpu.SemaphoreType.DMA
    return pl.pallas_call(
        functools.partial(body, cp, sp),
        out_shape=jax.ShapeDtypeStruct((tok, q_width), jnp.bfloat16),
        in_specs=[pl.BlockSpec(memory_space=pltpu.SMEM)] + [anywhere] * 3,
        out_specs=anywhere,
        scratch_shapes=[
            pltpu.VMEM((CHUNKS, sp, tok, qcols // CHUNKS), jnp.bfloat16),
            pltpu.VMEM((cp, group, HEAD_WIDTH), jnp.bfloat16),
            pltpu.VMEM((cp, group, HEAD_WIDTH), jnp.bfloat16),
            pltpu.VMEM((CHUNKS, sp, tok, qcols // CHUNKS), jnp.bfloat16),
            pltpu.VMEM((HEAD_WIDTH, width), jnp.float32),
            pltpu.VMEM((HEAD_WIDTH, width), jnp.float32),
            dma((2 + 2 * CHUNKS,)), dma((2, sp)), dma((2, sp)), dma((CHUNKS, sp)), dma((CHUNKS, sp)),
            dma((2, cp, sp, dims)), dma((2, cp, sp)), dma((CHUNKS, sp)), dma((CHUNKS, sp)),
        ],
        compiler_params=pltpu.CompilerParams(
            collective_id=0, has_side_effects=True, vmem_limit_bytes=60 * 1024 * 1024),
    )(span_order, queries, key_vectors, value_matrix)


def solution(mesh):
    return jax.shard_map(
        per_device,
        mesh=mesh,
        in_specs=(P(("cp", "sp"), None), P(("cp", "sp"), None), P(("cp", "sp"), None), P()),
        out_specs=P(("cp", "sp"), None),
        check_vma=False,
    )
```
